32 devices in a mesh: dp: 4 (over x, core), ctx: 8 (over z, y).
Axes of the slice: x: 2, y: 2, z: 4, core: 2. Of those that a mesh axis runs over, the one named last changes fastest.
Arguments:
- queries: bfloat16 [4, 2048, 1024], P('dp', 'ctx'), may hold values from -4.5 to 4.5
- keys: bfloat16 [4, 2048, 1024], P('dp', 'ctx'), may hold values from -4.5 to 4.5
- values: bfloat16 [4, 2048, 1024], P('dp', 'ctx'), may hold values from -6 to 6
- out_grad: bfloat16 [4, 2048, 2048], P('dp', 'ctx'), may hold values from -6 to 6
- chosen: int32 [4, 8], P('dp'), may hold values from -1 to 15, as said below
- proj: bfloat16 [1024, 2048], P('ctx', 'dp'), may hold values from -0.1875 to 0.1875
Outputs:
- attn_out: bfloat16 [4, 2048, 2048], P('dp', 'ctx')
- q_grad: bfloat16 [4, 2048, 1024], P('dp', 'ctx')
- k_grad: bfloat16 [4, 2048, 1024], P('dp', 'ctx')
- v_grad: bfloat16 [4, 2048, 1024], P('dp', 'ctx')
- proj_grad: float32 [1024, 2048], P('ctx', 'dp')
The draws below stay inside these ranges and needn't reach their ends.
Inputs may be any that keep to these rules, and one draw needn't show every extreme that they name: chosen[d, c] is -1 or the index pos // 128 of one of the blocks that ctx index c stores (position spans c and 15 - c, of 1 block each); every sequence has one or more entries that are not -1.
All inputs are finite; a program needn't handle non-finite values.
Results may differ from the reference program's by a relative error of at most 0.023.
Values may be sent and summed in bfloat16 or wider, within the bound.
A program may use at most 192 MiB of HBM per device.

```python
import math
import jax
import jax.numpy as jnp
from jax import lax

DH = 128
DOUT = 2048
BLOCK = 128
SPAN_BLOCKS = 1
HEADS = 8
HD = 1024
TOK_DEV = 256
SEQ = 2048
SLOTS = 1024
N_DP = 4
N_CTX = 8


def base_field(key, salt):
    inner = jax.random.fold_in(key, salt)
    field = jnp.clip(jax.random.normal(inner, (N_DP, SEQ, HD)), -4.5, 4.5)
    return field


def draw_queries(key, part):
    field = base_field(key, 1)
    return field.astype(jnp.bfloat16)


def draw_keys(key, part):
    field = base_field(key, 2)
    return field.astype(jnp.bfloat16)


def draw_chosen(key, part):
    ctx_ids = jnp.arange(N_CTX, dtype=jnp.int32)[None, :]
    pick = jax.random.randint(jax.random.fold_in(key, 11), (N_DP, N_CTX), 0, 2 * SPAN_BLOCKS)
    span_id = jnp.where(pick < SPAN_BLOCKS, ctx_ids, 2 * N_CTX - 1 - ctx_ids)
    block_id = span_id * SPAN_BLOCKS + pick % SPAN_BLOCKS
    active = jax.random.randint(jax.random.fold_in(key, 12), (N_DP, N_CTX), 0, 5) < 3
    forced = jax.random.randint(jax.random.fold_in(key, 13), (N_DP, 1), 0, N_CTX)
    active = active | (ctx_ids == forced)
    return jnp.where(active, block_id, -1).astype(jnp.int32)


def with_spikes(drawn, stream_key, source, target, blocks, factor):
    def block_of(position):
        return (jnp.arange(drawn.shape[position]) // (drawn.shape[position] // blocks)).reshape((-1,) + (1,) * (drawn.ndim - 1 - position))

    first = jax.random.permutation(stream_key, blocks)[block_of(target)]
    second = (block_of(target) + blocks // 2) % blocks
    return jnp.where((block_of(source) == first) | (block_of(source) == second), factor * drawn, drawn)


def shard_levels(own_key, extent, pieces, low, top_value):
    loudness, own = 1.0, jax.random.fold_in(own_key, 6)
    for axis_at, parts in pieces:
        draws = jnp.exp(jax.random.uniform(jax.random.fold_in(own, axis_at), (parts,), jnp.float32, low / len(pieces), top_value / len(pieces)))
        loudness = loudness * jnp.repeat(draws, extent[axis_at] // parts).reshape([-1 if axis == axis_at else 1 for axis in range(len(extent))])
    return loudness


def noise(own_key, dims, spread, reach, shards=(), held_as=jnp.bfloat16):
    loudness = shard_levels(own_key, dims, shards, -0.22, 0.18) if shards else 1.0
    drawn = jax.random.normal(own_key, dims, jnp.float32) * spread * loudness
    return jnp.minimum(jnp.maximum(drawn, -reach), reach).astype(held_as)


def heavy_noise(own_key, dims, width, limit, cuts, heavy, kind=jnp.bfloat16):
    drawn = width * jax.random.normal(own_key, dims, jnp.float32)
    if cuts:
        drawn = drawn * shard_levels(own_key, dims, cuts, -0.22, 0.18)
    return jnp.clip(with_spikes(drawn, jax.random.fold_in(own_key, 3), *heavy), -limit, limit).astype(kind)


def setup_inputs(seed: int = 0) -> dict:
    key_of = jax.random.split(jax.random.key(seed), 7)
    queries = draw_queries(jax.random.fold_in(key_of[6], 71), 0)
    keys = draw_keys(jax.random.fold_in(key_of[6], 71), 0)
    values = noise(key_of[2], (N_DP, SEQ, HD), 1.0, 6.0, ((0, 4), (1, 8)))
    out_grad = heavy_noise(key_of[3], (N_DP, SEQ, DOUT), 1.0, 6.0, ((0, 4), (1, 8)), (0, 2, 4, 2.0))
    chosen = draw_chosen(jax.random.fold_in(key_of[6], 71), 0)
    proj = noise(key_of[5], (HD, DOUT), HD ** -0.5, 0.1875, ((0, 8), (1, 4)))
    return dict(queries=queries, keys=keys, values=values, out_grad=out_grad, chosen=chosen, proj=proj)


def slot_rows(picked):
    half_rows = TOK_DEV // 2
    ctx_ids = jnp.arange(N_CTX, dtype=jnp.int32)
    live_pick = picked >= 0
    safe_pick = jnp.where(live_pick, picked, 0).astype(jnp.int32)
    first_pos = safe_pick * BLOCK
    span_id = first_pos // half_rows
    local_row = jnp.where(span_id == ctx_ids, first_pos % half_rows, half_rows + first_pos % half_rows)
    local_row = jnp.where(live_pick, local_row, 0).astype(jnp.int32)
    offsets = jnp.arange(BLOCK, dtype=jnp.int32)
    src_rows = (ctx_ids[:, None] * TOK_DEV + local_row[:, None] + offsets[None, :]).reshape(SLOTS).astype(jnp.int32)
    slot_pos = (safe_pick[:, None] * BLOCK + offsets[None, :]).reshape(SLOTS).astype(jnp.int32)
    slot_live = jnp.repeat(live_pick, BLOCK)
    return (src_rows, slot_pos, slot_live)

def head_probs(head_q, head_k, allowed):
    scores = jnp.dot(head_q, head_k.T, preferred_element_type=jnp.float32) * (1.0 / math.sqrt(DH))
    masked = jnp.where(allowed, scores, -1e+30)
    row_max = lax.optimization_barrier(jnp.max(masked, axis=1, keepdims=True))
    exp_terms = jnp.where(allowed, jnp.exp(masked - row_max), 0.0)
    return exp_terms / lax.optimization_barrier(jnp.sum(exp_terms, axis=1, keepdims=True))

def head_forward(head_q, head_k, head_v, allowed):
    attn_prob = head_probs(head_q, head_k, allowed)
    return jnp.dot(attn_prob.astype(jnp.bfloat16), head_v, preferred_element_type=jnp.float32).astype(jnp.bfloat16)

def head_backward(head_q, head_k, head_v, head_a, head_g, allowed):
    attn_prob = head_probs(head_q, head_k, allowed)
    prob_b = attn_prob.astype(jnp.bfloat16)
    row_delta = lax.optimization_barrier(jnp.sum(head_g.astype(jnp.float32) * head_a.astype(jnp.float32), axis=1, keepdims=True))
    prob_grad = jnp.dot(head_g, head_v.T, preferred_element_type=jnp.float32)
    score_grad = (attn_prob * (prob_grad - row_delta)).astype(jnp.bfloat16)
    score_scale = 1.0 / math.sqrt(DH)
    grad_q = (jnp.dot(score_grad, head_k, preferred_element_type=jnp.float32) * score_scale).astype(jnp.bfloat16)
    grad_k = (jnp.dot(score_grad.T, head_q, preferred_element_type=jnp.float32) * score_scale).astype(jnp.bfloat16)
    grad_v = jnp.dot(prob_b.T, head_g, preferred_element_type=jnp.float32).astype(jnp.bfloat16)
    return (grad_q, grad_k, grad_v)

def split_heads(block_rows):
    return block_rows.reshape(SLOTS, HEADS, DH).transpose(1, 0, 2)

def join_heads(block_rows):
    return block_rows.transpose(1, 0, 2).reshape(SLOTS, HD)

def one_sequence(seq_query, seq_key, seq_value, seq_grad, picked, proj):
    src_rows, slot_pos, slot_live = slot_rows(picked)
    live_col = slot_live[:, None]
    zero_bf = jnp.zeros((), jnp.bfloat16)
    query_slots = jnp.where(live_col, seq_query[src_rows], zero_bf)
    key_slots = jnp.where(live_col, seq_key[src_rows], zero_bf)
    value_slots = jnp.where(live_col, seq_value[src_rows], zero_bf)
    grad_slots = jnp.where(live_col, seq_grad[src_rows], zero_bf)
    slot_ids = jnp.arange(SLOTS, dtype=jnp.int32)
    allowed = live_col & slot_live[None, :] & (slot_pos[None, :] <= slot_pos[:, None]) | (slot_ids[:, None] == slot_ids[None, :])
    heads_q = split_heads(query_slots)
    heads_k = split_heads(key_slots)
    heads_v = split_heads(value_slots)

    def forward_one(triple):
        return head_forward(triple[0], triple[1], triple[2], allowed)
    attn_heads = lax.map(forward_one, (heads_q, heads_k, heads_v))
    attn = join_heads(attn_heads)
    mixed = jnp.dot(attn, proj, preferred_element_type=jnp.float32).astype(jnp.bfloat16)
    attn_grad = jnp.dot(grad_slots, proj.T, preferred_element_type=jnp.float32).astype(jnp.bfloat16)
    weight_term = jnp.dot(attn.T, grad_slots, preferred_element_type=jnp.float32)

    def backward_one(group):
        return head_backward(group[0], group[1], group[2], group[3], group[4], allowed)
    grad_q, grad_k, grad_v = lax.map(backward_one, (heads_q, heads_k, heads_v, attn_heads, split_heads(attn_grad)))
    out_rows = jnp.zeros((SEQ, DOUT), jnp.bfloat16).at[src_rows].set(mixed)
    blank = jnp.zeros((SEQ, HD), jnp.bfloat16)
    q_rows = blank.at[src_rows].set(join_heads(grad_q))
    k_rows = blank.at[src_rows].set(join_heads(grad_k))
    v_rows = blank.at[src_rows].set(join_heads(grad_v))
    return ((out_rows, q_rows, k_rows, v_rows), weight_term)

def reference(queries, keys, values, out_grad, chosen, proj):

    def scan_step(total, inputs):
        results, weight_term = one_sequence(inputs[0], inputs[1], inputs[2], inputs[3], inputs[4], proj)
        return (total + weight_term, results)
    total, stacked = lax.scan(scan_step, jnp.zeros((HD, DOUT), jnp.float32), (queries, keys, values, out_grad, chosen))
    return (stacked[0], stacked[1], stacked[2], stacked[3], total)
```

```python
import functools
import math

import jax
import jax.numpy as jnp
from jax import lax
from jax.experimental import pallas as pl
from jax.experimental.pallas import tpu as pltpu
from jax.sharding import PartitionSpec as P

BLOCK = 128
FAR = 1 << 30


def dot_nt(a, b):
    return lax.dot_general(a, b, (((1,), (1,)), ((), ())), preferred_element_type=jnp.float32)


def dot_nn(a, b):
    return lax.dot_general(a, b, (((1,), (0,)), ((), ())), preferred_element_type=jnp.float32)


def transposed(a):
    return a.astype(jnp.float32).T.astype(a.dtype)


def kernel(
    n, dn, scale,
    qkv, g, proj, kpos, qrow,
    dq_r, dkv_r, w_out, mix_r,
    qkv_r, g_r, proj_r, agp_s, agp_r, ag_s, ag_r, attn_s, attn_r, attn_d, attn_t,
    p_s, k_t, v_t, dq_s, dkv_s, dk_acc, dv_acc, w_s, w_r, mix_s,
    qkv_ss, qkv_rs, g_ss, g_rs, proj_ss, proj_rs, fwd_ss, agp_ss, agp_rs, ag_ss, ag_rs,
    attn_ss, attn_rs, ad_ss, ad_rs, dq_ss, dq_rs, dkv_ss, dkv_rs, w_ss, w_rs, mix_ss, mix_rs,
    loc,
):
    me = lax.axis_index("ctx")
    md = lax.axis_index("dp")
    bf16 = jnp.bfloat16
    block, dh = qkv.shape[2], qkv.shape[3]
    dc = proj.shape[1]
    slots = n * block
    width = 2 * block
    steps = n // 2

    def ctx_copy(src, dst, ss, rs, peer):
        return pltpu.make_async_remote_copy(
            src_ref=src, dst_ref=dst, send_sem=ss, recv_sem=rs,
            device_id={"ctx": peer}, device_id_type=pl.DeviceIdType.MESH)

    def dp_copy(src, dst, ss, rs, peer):
        return pltpu.make_async_remote_copy(
            src_ref=src, dst_ref=dst, send_sem=ss, recv_sem=rs,
            device_id={"dp": peer}, device_id_type=pl.DeviceIdType.MESH)

    ctx_peers = [lax.rem(me + s, n) for s in range(1, n)]
    dp_peers = [lax.rem(md + s, dn) for s in range(1, dn)]

    barrier = pltpu.get_barrier_semaphore()
    for peer in ctx_peers:
        pl.semaphore_signal(barrier, inc=1, device_id={"ctx": peer}, device_id_type=pl.DeviceIdType.MESH)
    for peer in dp_peers:
        pl.semaphore_signal(barrier, inc=1, device_id={"dp": peer}, device_id_type=pl.DeviceIdType.MESH)

    own = [
        pltpu.make_async_copy(qkv.at[me], qkv_r.at[me], loc.at[0]),
        pltpu.make_async_copy(g.at[md], g_r.at[md], loc.at[1]),
        pltpu.make_async_copy(proj, proj_r.at[me], loc.at[2]),
    ]
    for copy in own:
        copy.start()
    pl.semaphore_wait(barrier, n - 1 + dn - 1)

    pair = me + 1 - 2 * lax.rem(me, 2)
    far = [lax.rem(me + 2 * s, n) for s in range(1, n // 2)]
    sends = []

    def go(copy):
        copy.start()
        sends.append(copy)

    for peer in far + [pair]:
        go(ctx_copy(proj, proj_r.at[me], proj_ss.at[peer], proj_rs.at[me], peer))
    for peer in dp_peers:
        go(dp_copy(g.at[peer], g_r.at[md], g_ss.at[peer], g_rs.at[md], peer))
    for peer in ctx_peers:
        go(ctx_copy(qkv.at[peer], qkv_r.at[me], qkv_ss.at[peer], qkv_rs.at[me], peer))
    for copy in own:
        copy.wait()

    def ctx_arrived(buf, ss, rs, peer):
        ctx_copy(buf.at[peer], buf.at[peer], ss.at[peer], rs.at[peer], peer).wait_recv()

    def dp_arrived(buf, ss, rs, peer):
        dp_copy(buf.at[peer], buf.at[peer], ss.at[peer], rs.at[peer], peer).wait_recv()

    for peer in far:
        ctx_arrived(proj_r, proj_ss, proj_rs, peer)
        go(ctx_copy(proj_r.at[peer], proj_r.at[peer], fwd_ss.at[peer], proj_rs.at[peer], pair))
    for peer in [pair] + [lax.rem(pair + 2 * s, n) for s in range(1, n // 2)]:
        ctx_arrived(proj_r, proj_ss, proj_rs, peer)
    for peer in dp_peers:
        dp_arrived(g_r, g_ss, g_rs, peer)

    def part_step(j, carry):
        heads = proj_r[pl.ds(2 * j, 2)].reshape(2 * dh, dc)
        out = dot_nt(g_r[...].reshape(dn * block, dc), heads).astype(bf16)
        agp_s[:, pl.ds(2 * j, 1)] = out[:, :dh].reshape(dn, 1, block, dh)
        agp_s[:, pl.ds(2 * j + 1, 1)] = out[:, dh:].reshape(dn, 1, block, dh)
        return carry

    lax.fori_loop(0, steps, part_step, 0)
    for peer in dp_peers:
        go(dp_copy(agp_s.at[peer], agp_r.at[md], agp_ss.at[peer], agp_rs.at[md], peer))

    for peer in ctx_peers:
        ctx_arrived(qkv_r, qkv_ss, qkv_rs, peer)
    k_t[...] = transposed(qkv_r[:, 1].reshape(slots, dh))
    v_t[...] = transposed(qkv_r[:, 2].reshape(slots, dh))

    for peer in dp_peers:
        dp_arrived(agp_r, agp_ss, agp_rs, peer)

    def sum_step(h, carry):
        total = agp_s[md, h].astype(jnp.float32)
        for peer in dp_peers:
            total = total + agp_r[peer, h].astype(jnp.float32)
        ag_s[h] = total.astype(bf16)
        return carry

    lax.fori_loop(0, n, sum_step, 0)
    for peer in ctx_peers:
        go(ctx_copy(ag_s.at[peer], ag_r.at[me], ag_ss.at[peer], ag_rs.at[me], peer))
    ag_r[me] = ag_s[me]

    def send_pair(i, src, dst, ss, rs, own_sem):
        for half in range(2):
            peer = 2 * i + half

            @pl.when(peer != me)
            def _():
                ctx_copy(src.at[peer], dst.at[me], ss.at[peer], rs.at[me], peer).start()

            @pl.when(peer == me)
            def _():
                pltpu.make_async_copy(src.at[peer], dst.at[peer], own_sem).start()

    def forward(i, carry):
        q = qkv_r[pl.ds(2 * i, 2), 0].reshape(width, dh)
        k = qkv_r[:, 1].reshape(slots, dh)
        scores = dot_nt(k, q) * scale
        key_pos = kpos[...]
        key_pos = jnp.concatenate([key_pos, key_pos], axis=1)
        same = lax.broadcasted_iota(jnp.int32, (slots, width), 0) == (
            lax.broadcasted_iota(jnp.int32, (slots, width), 1) + i * width)
        scores = jnp.where((key_pos <= qrow[i]) | same, scores, -1e30)
        e = jnp.exp(scores - jnp.max(scores, axis=0, keepdims=True))
        p = (e * (1.0 / jnp.sum(e, axis=0, keepdims=True))).astype(bf16)
        p_s[i] = p
        a_t = dot_nn(v_t[...], p)
        attn_t[i] = a_t.astype(bf16)
        attn_s[pl.ds(2 * i, 2)] = a_t.T.astype(bf16).reshape(2, block, dh)
        send_pair(i, attn_s, attn_r, attn_ss, attn_rs, loc.at[3])
        return carry

    lax.fori_loop(0, steps, forward, 0)

    for peer in ctx_peers:
        ctx_arrived(ag_r, ag_ss, ag_rs, peer)
    dk_acc[...] = jnp.zeros_like(dk_acc)
    dv_acc[...] = jnp.zeros_like(dv_acc)

    def backward(i, carry):
        q = qkv_r[pl.ds(2 * i, 2), 0].reshape(width, dh)
        v = qkv_r[:, 2].reshape(slots, dh)
        da = ag_r[pl.ds(2 * i, 2)].reshape(width, dh)
        delta = jnp.sum(da.astype(jnp.float32).T * attn_t[i].astype(jnp.float32), axis=0, keepdims=True)
        p = p_s[i]
        ds = (p.astype(jnp.float32) * (dot_nt(v, da) - delta)).astype(bf16)
        dq_t = dot_nn(k_t[...], ds) * scale
        dq_s[pl.ds(2 * i, 2)] = dq_t.T.astype(bf16).reshape(2, block, dh)
        send_pair(i, dq_s, dq_r, dq_ss, dq_rs, loc.at[4])
        dk_acc[...] += dot_nn(ds, q)
        dv_acc[...] += dot_nn(p, da)
        return carry

    early = steps // 2
    lax.fori_loop(0, early, backward, 0)
    for peer in ctx_peers:
        ctx_arrived(attn_r, attn_ss, attn_rs, peer)
    pltpu.make_async_copy(attn_s.at[me], attn_r.at[me], loc.at[3]).wait()
    for peer in dp_peers:
        go(dp_copy(attn_r, attn_d.at[md], ad_ss.at[peer], ad_rs.at[md], peer))
    own_attn = pltpu.make_async_copy(attn_r, attn_d.at[md], loc.at[5])
    own_attn.start()
    lax.fori_loop(early, steps, backward, 0)

    dkv_s[:, 0] = (dk_acc[...] * scale).astype(bf16).reshape(n, block, dh)
    dkv_s[:, 1] = dv_acc[...].astype(bf16).reshape(n, block, dh)
    for peer in ctx_peers:
        go(ctx_copy(dkv_s.at[peer], dkv_r.at[me], dkv_ss.at[peer], dkv_rs.at[me], peer))
    dkv_r[me] = dkv_s[me]

    own_attn.wait()
    for peer in dp_peers:
        dp_arrived(attn_d, ad_ss, ad_rs, peer)

    def weight_step(s, carry):
        h = lax.rem(me + s, n)
        heads = attn_d[:, h].reshape(dn * block, dh)
        w_s[h] = dot_nn(transposed(heads), g_r[...].reshape(dn * block, dc)).astype(bf16)

        @pl.when(s != 0)
        def _():
            ctx_copy(w_s.at[h], w_r.at[me], w_ss.at[h], w_rs.at[me], h).start()

        return carry

    lax.fori_loop(0, n, lambda s, carry: weight_step(n - 1 - s, carry), 0)

    def mix_step(j, carry):
        rows = jnp.concatenate(
            [attn_d[pl.ds(2 * j, 2), h].reshape(width, dh) for h in range(n)], axis=1)
        out = dot_nn(rows, proj_r[...].reshape(n * dh, dc))
        mix_s[pl.ds(2 * j, 2)] = out.astype(bf16).reshape(2, block, dc)
        return carry

    lax.fori_loop(0, dn // 2, mix_step, 0)
    for peer in dp_peers:
        go(dp_copy(mix_s.at[peer], mix_r.at[md], mix_ss.at[peer], mix_rs.at[md], peer))
    mix_r[md] = mix_s[md]

    pltpu.make_async_copy(dq_s.at[me], dq_r.at[me], loc.at[4]).wait()
    for peer in ctx_peers:
        ctx_arrived(dq_r, dq_ss, dq_rs, peer)
    for peer in ctx_peers:
        ctx_arrived(dkv_r, dkv_ss, dkv_rs, peer)
    for peer in ctx_peers:
        ctx_arrived(w_r, w_ss, w_rs, peer)
    total = w_s[me].astype(jnp.float32)
    for peer in ctx_peers:
        total = total + w_r[peer].astype(jnp.float32)
    w_out[...] = total
    for peer in dp_peers:
        dp_arrived(mix_r, mix_ss, mix_rs, peer)

    for copy in sends:
        copy.wait_send()
    for peer in ctx_peers:
        ctx_copy(attn_s.at[peer], attn_r.at[me], attn_ss.at[peer], attn_rs.at[me], peer).wait_send()
        ctx_copy(dq_s.at[peer], dq_r.at[me], dq_ss.at[peer], dq_rs.at[me], peer).wait_send()
        ctx_copy(w_s.at[peer], w_r.at[me], w_ss.at[peer], w_rs.at[me], peer).wait_send()


def shards(queries, keys, values, out_grad, chosen, proj):
    n = lax.axis_size("ctx")
    dn = lax.axis_size("dp")
    me = lax.axis_index("ctx")
    tokens = queries.shape[1]
    half_rows = tokens // 2
    picked = chosen[0]
    own_pick = lax.dynamic_index_in_dim(picked, me, 0, keepdims=False)
    own_live = own_pick >= 0
    first_pos = jnp.where(own_live, own_pick, 0) * BLOCK
    local_row = jnp.where(
        first_pos // half_rows == me,
        first_pos % half_rows,
        half_rows + first_pos % half_rows,
    )
    row_start = jnp.where(own_live, local_row, 0)

    def take_rows(source):
        slot_block = lax.dynamic_slice_in_dim(source[0], row_start, BLOCK, 0)
        return jnp.where(own_live, slot_block, jnp.zeros((), source.dtype))

    dh = queries.shape[2] // n
    dc = proj.shape[1]
    slots = n * BLOCK
    width = 2 * BLOCK
    steps = n // 2

    def by_head(rows):
        return rows.reshape(BLOCK, n, dh).transpose(1, 0, 2)

    qkv = jnp.stack([by_head(take_rows(x)) for x in (queries, keys, values)], axis=1)
    g = take_rows(out_grad).reshape(BLOCK, dn, dc).transpose(1, 0, 2)

    offsets = jnp.arange(BLOCK, dtype=jnp.int32)
    live = picked >= 0
    pos = (picked[:, None] * BLOCK + offsets[None, :])
    key_pos = jnp.where(live[:, None], pos, FAR).reshape(slots)
    query_pos = jnp.where(live[:, None], pos, -1).reshape(steps, 1, width)
    key_pos = jnp.broadcast_to(key_pos[:, None], (slots, BLOCK))

    bf16, f32 = jnp.bfloat16, jnp.float32
    sem = pltpu.SemaphoreType.DMA
    vm = pltpu.VMEM
    blocks = (n, BLOCK, dh)
    scratch = [
        vm((n, 3, BLOCK, dh), bf16), vm((dn, BLOCK, dc), bf16), vm((n, dh, dc), bf16),
        vm((dn,) + blocks, bf16), vm((dn,) + blocks, bf16), vm(blocks, bf16), vm(blocks, bf16),
        vm(blocks, bf16), vm(blocks, bf16), vm((dn,) + blocks, bf16), vm((steps, dh, width), bf16),
        vm((steps, slots, width), bf16), vm((dh, slots), bf16), vm((dh, slots), bf16),
        vm(blocks, bf16), vm((n, 2, BLOCK, dh), bf16), vm((slots, dh), f32), vm((slots, dh), f32),
        vm((n, dh, dc), bf16), vm((n, dh, dc), bf16), vm((dn, BLOCK, dc), bf16),
    ]
    c, d = sem((n,)), sem((dn,))
    sems = [c, c, d, d, c, c, c, d, d, c, c, c, c, d, d, c, c, c, c, c, c, d, d, sem((6,))]
    dq, dkv, proj_grad, mixed = pl.pallas_call(
        functools.partial(kernel, n, dn, 1.0 / math.sqrt(dh)),
        out_shape=(
            jax.ShapeDtypeStruct(blocks, bf16),
            jax.ShapeDtypeStruct((n, 2, BLOCK, dh), bf16),
            jax.ShapeDtypeStruct((dh, dc), f32),
            jax.ShapeDtypeStruct((dn, BLOCK, dc), bf16),
        ),
        in_specs=[pl.BlockSpec(memory_space=pltpu.VMEM)] * 5,
        out_specs=[pl.BlockSpec(memory_space=pltpu.VMEM)] * 4,
        scratch_shapes=scratch + sems,
        compiler_params=pltpu.CompilerParams(
            collective_id=0, has_side_effects=True, vmem_limit_bytes=60 * 1024 * 1024),
    )(qkv, g, proj, key_pos, query_pos)

    count = tokens // BLOCK
    here = (jnp.arange(count, dtype=jnp.int32) == row_start // BLOCK) & own_live

    def place(rows):
        out = jnp.where(here[:, None, None], rows[None], jnp.zeros((), rows.dtype))
        return out.reshape(1, tokens, rows.shape[1])

    def rows_of(parts):
        return parts.transpose(1, 0, 2).reshape(BLOCK, parts.shape[0] * parts.shape[2])

    return (
        place(rows_of(mixed)),
        place(rows_of(dq)),
        place(rows_of(dkv[:, 0])),
        place(rows_of(dkv[:, 1])),
        proj_grad,
    )


def solution(mesh):
    rows = P("dp", "ctx", None)
    return jax.shard_map(
        shards,
        mesh=mesh,
        in_specs=(rows, rows, rows, rows, P("dp", None), P("ctx", "dp")),
        out_specs=(rows, rows, rows, rows, P("ctx", "dp")),
        check_vma=False,
    )
```

```python
import functools
import math

import jax
import jax.numpy as jnp
from jax import lax
from jax.experimental import pallas as pl
from jax.experimental.pallas import tpu as pltpu
from jax.sharding import PartitionSpec as P

BLOCK = 128
FAR = 1 << 30


def dot_nt(a, b):
    return lax.dot_general(a, b, (((1,), (1,)), ((), ())), preferred_element_type=jnp.float32)


def dot_nn(a, b):
    return lax.dot_general(a, b, (((1,), (0,)), ((), ())), preferred_element_type=jnp.float32)


def transposed(a):
    return a.astype(jnp.float32).T.astype(a.dtype)


def block_marks(picked, me, count):
    entry = picked[0, me]
    spans = count // 2
    index = jnp.maximum(entry, 0)
    local = jnp.where(index // spans == me, index % spans, spans + index % spans)
    local = jnp.where(entry >= 0, local, -1)
    return [jnp.where(local == j, 1.0, 0.0) for j in range(count)]


def place_kernel(n, dn, count, picked, mix, dq, dkv, w, out, q_out, k_out, v_out, w_out):
    marks = block_marks(picked, lax.axis_index("ctx"), count)
    block, dh, dc = dq.shape[1], dq.shape[2], mix.shape[2]
    for j, mark in enumerate(marks):
        rows = slice(j * block, (j + 1) * block)
        for h in range(n):
            cols = slice(h * dh, (h + 1) * dh)
            q_out[rows, cols] = (dq[h].astype(jnp.float32) * mark).astype(q_out.dtype)
            k_out[rows, cols] = (dkv[h, 0].astype(jnp.float32) * mark).astype(k_out.dtype)
            v_out[rows, cols] = (dkv[h, 1].astype(jnp.float32) * mark).astype(v_out.dtype)
        for d in range(dn):
            cols = slice(d * dc, (d + 1) * dc)
            out[rows, cols] = (mix[d].astype(jnp.float32) * mark).astype(out.dtype)
    w_out[...] = w[...]


def kernel(
    n, dn, scale,
    picked, q_in, k_in, v_in, g_in, proj,
    dq_r, dkv_r, w_out, mix_r,
    qkv, g, kpos, qkv_r, g_r, proj_r, agp_s, agp_r, ag_s, ag_r, attn_s, attn_r, attn_d, attn_t,
    p_s, k_t, v_t, dq_s, dkv_s, dk_acc, dv_acc, w_s, w_y, w_r, mix_s,
    qkv_ss, qkv_rs, g_ss, g_rs, proj_ss, proj_rs, fwd_ss, agp_ss, agp_rs, ag_ss, ag_rs,
    attn_ss, attn_rs, ad_ss, ad_rs, ad_fs, dq_ss, dq_rs, dkv_ss, dkv_rs, w_ss, wy_rs, w_rs, mix_ss, mix_rs,
    loc,
):
    me = lax.axis_index("ctx")
    md = lax.axis_index("dp")
    bf16 = jnp.bfloat16
    block, dh = qkv.shape[2], qkv.shape[3]
    dc = proj.shape[1]
    slots = n * block
    width = 2 * block
    steps = n // 2

    def ctx_copy(src, dst, ss, rs, peer):
        return pltpu.make_async_remote_copy(
            src_ref=src, dst_ref=dst, send_sem=ss, recv_sem=rs,
            device_id={"ctx": peer}, device_id_type=pl.DeviceIdType.MESH)

    def dp_copy(src, dst, ss, rs, peer):
        return pltpu.make_async_remote_copy(
            src_ref=src, dst_ref=dst, send_sem=ss, recv_sem=rs,
            device_id={"dp": peer}, device_id_type=pl.DeviceIdType.MESH)

    ctx_peers = [lax.rem(me + s, n) for s in range(1, n)]
    dp_peers = [lax.rem(md + s, dn) for s in range(1, dn)]

    barrier = pltpu.get_barrier_semaphore()
    for peer in ctx_peers:
        pl.semaphore_signal(barrier, inc=1, device_id={"ctx": peer}, device_id_type=pl.DeviceIdType.MESH)
    for peer in dp_peers:
        pl.semaphore_signal(barrier, inc=1, device_id={"dp": peer}, device_id_type=pl.DeviceIdType.MESH)

    own_proj = pltpu.make_async_copy(proj, proj_r.at[me], loc.at[2])
    own_proj.start()
    marks = block_marks(picked, me, q_in.shape[0] // block)

    def chosen_rows(ref, low, high):
        total = None
        for j, mark in enumerate(marks):
            term = ref[j * block:(j + 1) * block, low:high].astype(jnp.float32) * mark
            total = term if total is None else total + term
        return total.astype(bf16)

    pair = me + 1 - 2 * lax.rem(me, 2)
    far = [lax.rem(me + 2 * s, n) for s in range(1, n // 2)]
    pl.semaphore_wait(barrier, n - 1 + dn - 1)
    sends = []

    def go(copy):
        copy.start()
        sends.append(copy)

    for peer in far + [pair]:
        go(ctx_copy(proj, proj_r.at[me], proj_ss.at[peer], proj_rs.at[me], peer))
    for j in range(dn):
        g[j] = chosen_rows(g_in, j * dc, (j + 1) * dc)
    for peer in dp_peers:
        go(dp_copy(g.at[peer], g_r.at[md], g_ss.at[peer], g_rs.at[md], peer))
    g_r[md] = g[md]
    for t, ref in enumerate((q_in, k_in, v_in)):
        for h in range(n):
            qkv[h, t] = chosen_rows(ref, h * dh, (h + 1) * dh)
    qkv_r[me] = qkv[me]
    down = lax.broadcasted_iota(jnp.int32, (block, block), 0)
    for j in range(n):
        entry = picked[0, j]
        kpos[j * block:(j + 1) * block] = down + jnp.where(entry >= 0, entry * block, FAR)
    own_proj.wait()

    def ctx_arrived(buf, ss, rs, peer):
        ctx_copy(buf.at[peer], buf.at[peer], ss.at[peer], rs.at[peer], peer).wait_recv()

    def dp_arrived(buf, ss, rs, peer):
        dp_copy(buf.at[peer], buf.at[peer], ss.at[peer], rs.at[peer], peer).wait_recv()

    for peer in far:
        ctx_arrived(proj_r, proj_ss, proj_rs, peer)
        go(ctx_copy(proj_r.at[peer], proj_r.at[peer], fwd_ss.at[peer], proj_rs.at[peer], pair))
    for peer in ctx_peers:
        go(ctx_copy(qkv.at[peer], qkv_r.at[me], qkv_ss.at[peer], qkv_rs.at[me], peer))
    for peer in [pair] + [lax.rem(pair + 2 * s, n) for s in range(1, n // 2)]:
        ctx_arrived(proj_r, proj_ss, proj_rs, peer)
    for peer in dp_peers:
        dp_arrived(g_r, g_ss, g_rs, peer)

    def part_step(j, carry):
        heads = proj_r[pl.ds(2 * j, 2)].reshape(2 * dh, dc)
        out = dot_nt(g_r[...].reshape(dn * block, dc), heads).astype(bf16)
        agp_s[:, pl.ds(2 * j, 1)] = out[:, :dh].reshape(dn, 1, block, dh)
        agp_s[:, pl.ds(2 * j + 1, 1)] = out[:, dh:].reshape(dn, 1, block, dh)
        return carry

    lax.fori_loop(0, steps, part_step, 0)
    for peer in dp_peers:
        go(dp_copy(agp_s.at[peer], agp_r.at[md], agp_ss.at[peer], agp_rs.at[md], peer))

    for peer in ctx_peers:
        ctx_arrived(qkv_r, qkv_ss, qkv_rs, peer)
    k_t[...] = transposed(qkv_r[:, 1].reshape(slots, dh))
    v_t[...] = transposed(qkv_r[:, 2].reshape(slots, dh))

    for peer in dp_peers:
        dp_arrived(agp_r, agp_ss, agp_rs, peer)

    def sum_step(h, carry):
        total = agp_s[md, h].astype(jnp.float32)
        for peer in dp_peers:
            total = total + agp_r[peer, h].astype(jnp.float32)
        ag_s[h] = total.astype(bf16)
        return carry

    lax.fori_loop(0, n, sum_step, 0)
    for peer in ctx_peers:
        go(ctx_copy(ag_s.at[peer], ag_r.at[me], ag_ss.at[peer], ag_rs.at[me], peer))
    ag_r[me] = ag_s[me]

    def send_pair(i, src, dst, ss, rs, own_sem):
        for half in range(2):
            peer = 2 * i + half

            @pl.when(peer != me)
            def _():
                ctx_copy(src.at[peer], dst.at[me], ss.at[peer], rs.at[me], peer).start()

            @pl.when(peer == me)
            def _():
                pltpu.make_async_copy(src.at[peer], dst.at[peer], own_sem).start()

    def forward(i, carry):
        q = qkv_r[pl.ds(2 * i, 2), 0].reshape(width, dh)
        k = qkv_r[:, 1].reshape(slots, dh)
        scores = dot_nt(k, q) * scale
        key_pos = kpos[...]
        key_pos = jnp.concatenate([key_pos, key_pos], axis=1)
        same = lax.broadcasted_iota(jnp.int32, (slots, width), 0) == (
            lax.broadcasted_iota(jnp.int32, (slots, width), 1) + i * width)
        lane = lax.broadcasted_iota(jnp.int32, (1, width), 1)
        first, second = picked[0, 2 * i], picked[0, 2 * i + 1]
        first = jnp.where(first >= 0, first * block, -FAR)
        second = jnp.where(second >= 0, (second - 1) * block, -FAR)
        query_pos = lane + jnp.where(lane < block, first, second)
        scores = jnp.where((key_pos <= query_pos) | same, scores, -1e30)
        e = jnp.exp(scores - jnp.max(scores, axis=0, keepdims=True))
        p = (e * (1.0 / jnp.sum(e, axis=0, keepdims=True))).astype(bf16)
        p_s[i] = p
        a_t = dot_nn(v_t[...], p)
        attn_t[i] = a_t.astype(bf16)
        attn_s[pl.ds(2 * i, 2)] = a_t.T.astype(bf16).reshape(2, block, dh)
        send_pair(i, attn_s, attn_r, attn_ss, attn_rs, loc.at[3])
        return carry

    lax.fori_loop(0, steps, forward, 0)

    for peer in ctx_peers:
        ctx_arrived(ag_r, ag_ss, ag_rs, peer)
    dk_acc[...] = jnp.zeros_like(dk_acc)
    dv_acc[...] = jnp.zeros_like(dv_acc)

    def backward(i, carry):
        q = qkv_r[pl.ds(2 * i, 2), 0].reshape(width, dh)
        v = qkv_r[:, 2].reshape(slots, dh)
        da = ag_r[pl.ds(2 * i, 2)].reshape(width, dh)
        delta = jnp.sum(da.astype(jnp.float32).T * attn_t[i].astype(jnp.float32), axis=0, keepdims=True)
        p = p_s[i]
        ds = (p.astype(jnp.float32) * (dot_nt(v, da) - delta)).astype(bf16)
        dq_t = dot_nn(k_t[...], ds) * scale
        dq_s[pl.ds(2 * i, 2)] = dq_t.T.astype(bf16).reshape(2, block, dh)
        send_pair(i, dq_s, dq_r, dq_ss, dq_rs, loc.at[4])
        dk_acc[...] += dot_nn(ds, q)
        dv_acc[...] += dot_nn(p, da)
        return carry

    early = steps // 2
    lax.fori_loop(0, early, backward, 0)
    for peer in ctx_peers:
        ctx_arrived(attn_r, attn_ss, attn_rs, peer)
    pltpu.make_async_copy(attn_s.at[me], attn_r.at[me], loc.at[3]).wait()
    twin = md + 1 - 2 * lax.rem(md, 2)
    dp_far = [lax.rem(md + 2 * s, dn) for s in range(1, dn // 2)]
    for peer in dp_far + [twin]:
        go(dp_copy(attn_r, attn_d.at[md], ad_ss.at[peer], ad_rs.at[md], peer))
    own_attn = pltpu.make_async_copy(attn_r, attn_d.at[md], loc.at[5])
    own_attn.start()
    lax.fori_loop(early, steps, backward, 0)

    dkv_s[:, 0] = (dk_acc[...] * scale).astype(bf16).reshape(n, block, dh)
    dkv_s[:, 1] = dv_acc[...].astype(bf16).reshape(n, block, dh)
    for peer in ctx_peers:
        go(ctx_copy(dkv_s.at[peer], dkv_r.at[me], dkv_ss.at[peer], dkv_rs.at[me], peer))
    dkv_r[me] = dkv_s[me]

    own_attn.wait()
    for peer in dp_far:
        dp_arrived(attn_d, ad_ss, ad_rs, peer)
        go(dp_copy(attn_d.at[peer], attn_d.at[peer], ad_fs.at[peer], ad_rs.at[peer], twin))
    for peer in [twin] + [lax.rem(twin + 2 * s, dn) for s in range(1, dn // 2)]:
        dp_arrived(attn_d, ad_ss, ad_rs, peer)

    def weight(h):
        heads = attn_d[:, h].reshape(dn * block, dh)
        return dot_nn(transposed(heads), g_r[...].reshape(dn * block, dc))

    side = lax.rem(me, 2)
    row = me // 2
    orders = [lax.rem(row + s, n // 2) for s in range(1, n // 2)] + [row]
    for a in orders:
        h = 2 * a + 1 - side
        w_s[h] = weight(h).astype(bf16)
        go(ctx_copy(w_s.at[h], w_y.at[a], w_ss.at[h], wy_rs.at[a], pair))

    def mix_step(j, carry):
        rows = jnp.concatenate(
            [attn_d[pl.ds(2 * j, 2), h].reshape(width, dh) for h in range(n)], axis=1)
        out = dot_nn(rows, proj_r[...].reshape(n * dh, dc))
        mix_s[pl.ds(2 * j, 2)] = out.astype(bf16).reshape(2, block, dc)
        return carry

    lax.fori_loop(0, dn // 2, mix_step, 0)
    for peer in dp_peers:
        go(dp_copy(mix_s.at[peer], mix_r.at[md], mix_ss.at[peer], mix_rs.at[md], peer))
    mix_r[md] = mix_s[md]

    for a in orders:
        h = 2 * a + side
        total = weight(h)
        ctx_copy(w_y.at[a], w_y.at[a], w_ss.at[h], wy_rs.at[a], pair).wait_recv()
        total = total + w_y[a].astype(jnp.float32)
        if a is row:
            w_out[...] = total
        else:
            w_s[h] = total.astype(bf16)
            go(ctx_copy(w_s.at[h], w_r.at[row], w_ss.at[h], w_rs.at[row], h))

    pltpu.make_async_copy(dq_s.at[me], dq_r.at[me], loc.at[4]).wait()
    for peer in ctx_peers:
        ctx_arrived(dq_r, dq_ss, dq_rs, peer)
    for peer in ctx_peers:
        ctx_arrived(dkv_r, dkv_ss, dkv_rs, peer)
    for a in orders[:-1]:
        ctx_copy(w_r.at[a], w_r.at[a], w_ss.at[a], w_rs.at[a], pair).wait_recv()
        w_out[...] += w_r[a].astype(jnp.float32)
    for peer in dp_peers:
        dp_arrived(mix_r, mix_ss, mix_rs, peer)

    for copy in sends:
        copy.wait_send()
    for peer in ctx_peers:
        ctx_copy(attn_s.at[peer], attn_r.at[me], attn_ss.at[peer], attn_rs.at[me], peer).wait_send()
        ctx_copy(dq_s.at[peer], dq_r.at[me], dq_ss.at[peer], dq_rs.at[me], peer).wait_send()


def shards(queries, keys, values, out_grad, chosen, proj):
    n = lax.axis_size("ctx")
    dn = lax.axis_size("dp")
    tokens = queries.shape[1]
    dh = queries.shape[2] // n
    dc = proj.shape[1]
    slots = n * BLOCK
    width = 2 * BLOCK
    steps = n // 2
    bf16, f32 = jnp.bfloat16, jnp.float32
    sem = pltpu.SemaphoreType.DMA
    vm = pltpu.VMEM
    blocks = (n, BLOCK, dh)
    scratch = [
        vm((n, 3, BLOCK, dh), bf16), vm((dn, BLOCK, dc), bf16), vm((slots, BLOCK), jnp.int32),
        vm((n, 3, BLOCK, dh), bf16), vm((dn, BLOCK, dc), bf16), vm((n, dh, dc), bf16),
        vm((dn,) + blocks, bf16), vm((dn,) + blocks, bf16), vm(blocks, bf16), vm(blocks, bf16),
        vm(blocks, bf16), vm(blocks, bf16), vm((dn,) + blocks, bf16), vm((steps, dh, width), bf16),
        vm((steps, slots, width), bf16), vm((dh, slots), bf16), vm((dh, slots), bf16),
        vm(blocks, bf16), vm((n, 2, BLOCK, dh), bf16), vm((slots, dh), f32), vm((slots, dh), f32),
        vm((n, dh, dc), bf16), vm((n // 2, dh, dc), bf16), vm((n // 2, dh, dc), bf16), vm((dn, BLOCK, dc), bf16),
    ]
    c, d = sem((n,)), sem((dn,))
    sems = [c, c, d, d, c, c, c, d, d, c, c, c, c, d, d, d, c, c, c, c, c, c, c, d, d, sem((6,))]
    vmem = pl.BlockSpec(memory_space=pltpu.VMEM)
    smem = pl.BlockSpec(memory_space=pltpu.SMEM)
    dq, dkv, weight_grad, mixed = pl.pallas_call(
        functools.partial(kernel, n, dn, 1.0 / math.sqrt(dh)),
        out_shape=(
            jax.ShapeDtypeStruct(blocks, bf16),
            jax.ShapeDtypeStruct((n, 2, BLOCK, dh), bf16),
            jax.ShapeDtypeStruct((dh, dc), f32),
            jax.ShapeDtypeStruct((dn, BLOCK, dc), bf16),
        ),
        in_specs=[smem] + [vmem] * 5,
        out_specs=[pl.BlockSpec(memory_space=pltpu.VMEM)] * 4,
        scratch_shapes=scratch + sems,
        compiler_params=pltpu.CompilerParams(
            collective_id=0, has_side_effects=True, vmem_limit_bytes=60 * 1024 * 1024),
    )(chosen, queries[0], keys[0], values[0], out_grad[0], proj)

    wide = jax.ShapeDtypeStruct((tokens, dn * dc), bf16)
    thin = jax.ShapeDtypeStruct((tokens, n * dh), bf16)
    out, q_grad, k_grad, v_grad, proj_grad = pl.pallas_call(
        functools.partial(place_kernel, n, dn, tokens // BLOCK),
        out_shape=(wide, thin, thin, thin, jax.ShapeDtypeStruct((dh, dc), f32)),
        in_specs=[smem] + [vmem] * 4,
        out_specs=[vmem] * 5,
    )(chosen, mixed, dq, dkv, weight_grad)
    return out[None], q_grad[None], k_grad[None], v_grad[None], proj_grad


def solution(mesh):
    rows = P("dp", "ctx", None)
    return jax.shard_map(
        shards,
        mesh=mesh,
        in_specs=(rows, rows, rows, rows, P("dp", None), P("ctx", "dp")),
        out_specs=(rows, rows, rows, rows, P("ctx", "dp")),
        check_vma=False,
    )
```

```python
import functools
import math

import jax
import jax.numpy as jnp
from jax import lax
from jax.experimental import pallas as pl
from jax.experimental.pallas import tpu as pltpu
from jax.sharding import PartitionSpec as P

BLOCK = 128
FAR = 1 << 30


def dot_nt(a, b):
    return lax.dot_general(a, b, (((1,), (1,)), ((), ())), preferred_element_type=jnp.float32)


def dot_nn(a, b):
    return lax.dot_general(a, b, (((1,), (0,)), ((), ())), preferred_element_type=jnp.float32)


def transposed(a):
    return a.astype(jnp.float32).T.astype(a.dtype)


def block_marks(picked, me, count):
    entry = picked[0, me]
    spans = count // 2
    index = jnp.maximum(entry, 0)
    local = jnp.where(index // spans == me, index % spans, spans + index % spans)
    local = jnp.where(entry >= 0, local, -1)
    return [jnp.where(local == j, 1.0, 0.0) for j in range(count)]


def place_kernel(n, dn, count, picked, mix, dq, dkv, w, out, q_out, k_out, v_out, w_out):
    marks = block_marks(picked, lax.axis_index("ctx"), count)
    block, dh, dc = dq.shape[1], dq.shape[2], mix.shape[2]
    for j, mark in enumerate(marks):
        rows = slice(j * block, (j + 1) * block)
        for h in range(n):
            cols = slice(h * dh, (h + 1) * dh)
            q_out[rows, cols] = (dq[h].astype(jnp.float32) * mark).astype(q_out.dtype)
            k_out[rows, cols] = (dkv[h, 0].astype(jnp.float32) * mark).astype(k_out.dtype)
            v_out[rows, cols] = (dkv[h, 1].astype(jnp.float32) * mark).astype(v_out.dtype)
        for d in range(dn):
            cols = slice(d * dc, (d + 1) * dc)
            out[rows, cols] = (mix[d].astype(jnp.float32) * mark).astype(out.dtype)
    w_out[...] = w[...]


def kernel(
    n, dn, scale,
    picked, q_in, k_in, v_in, g_in, proj,
    dq_r, dkv_r, w_out, mix_r,
    qkv, g, kpos, qkv_r, g_r, proj_r, agp_s, agp_r, ag_s, ag_r, attn_s, attn_r, attn_d, attn_t,
    p_s, k_t, v_t, dq_s, dkv_s, dk_acc, dv_acc, w_s, w_y, w_r, mix_s,
    qkv_ss, qkv_rs, g_ss, g_rs, proj_ss, proj_rs, fwd_ss, agp_ss, agp_rs, ag_ss, ag_rs,
    attn_ss, attn_rs, ad_ss, ad_rs, ad_fs, dq_ss, dq_rs, dkv_ss, dkv_rs, w_ss, wy_rs, w_rs, mix_ss, mix_rs,
    loc,
):
    me = lax.axis_index("ctx")
    md = lax.axis_index("dp")
    bf16 = jnp.bfloat16
    block, dh = qkv.shape[2], qkv.shape[3]
    dc = proj.shape[1]
    slots = n * block
    width = 2 * block
    steps = n // 2

    def ctx_copy(src, dst, ss, rs, peer):
        return pltpu.make_async_remote_copy(
            src_ref=src, dst_ref=dst, send_sem=ss, recv_sem=rs,
            device_id={"ctx": peer}, device_id_type=pl.DeviceIdType.MESH)

    def dp_copy(src, dst, ss, rs, peer):
        return pltpu.make_async_remote_copy(
            src_ref=src, dst_ref=dst, send_sem=ss, recv_sem=rs,
            device_id={"dp": peer}, device_id_type=pl.DeviceIdType.MESH)

    ctx_peers = [lax.rem(me + s, n) for s in range(1, n)]
    dp_peers = [lax.rem(md + s, dn) for s in range(1, dn)]

    barrier = pltpu.get_barrier_semaphore()
    for peer in ctx_peers:
        pl.semaphore_signal(barrier, inc=1, device_id={"ctx": peer}, device_id_type=pl.DeviceIdType.MESH)
    for peer in dp_peers:
        pl.semaphore_signal(barrier, inc=1, device_id={"dp": peer}, device_id_type=pl.DeviceIdType.MESH)

    own_proj = pltpu.make_async_copy(proj, proj_r.at[me], loc.at[2])
    own_proj.start()
    marks = block_marks(picked, me, q_in.shape[0] // block)

    def chosen_rows(ref, low, high):
        total = None
        for j, mark in enumerate(marks):
            term = ref[j * block:(j + 1) * block, low:high].astype(jnp.float32) * mark
            total = term if total is None else total + term
        return total.astype(bf16)

    pair = me + 1 - 2 * lax.rem(me, 2)
    far = [lax.rem(me + 2 * s, n) for s in range(1, n // 2)]
    pl.semaphore_wait(barrier, n - 1 + dn - 1)
    sends = []

    def go(copy):
        copy.start()
        sends.append(copy)

    for peer in far + [pair]:
        go(ctx_copy(proj, proj_r.at[me], proj_ss.at[peer], proj_rs.at[me], peer))
    for j in range(dn):
        g[j] = chosen_rows(g_in, j * dc, (j + 1) * dc)
    for peer in dp_peers:
        go(dp_copy(g.at[peer], g_r.at[md], g_ss.at[peer], g_rs.at[md], peer))
    g_r[md] = g[md]
    for t, ref in enumerate((q_in, k_in, v_in)):
        for h in range(n):
            qkv[h, t] = chosen_rows(ref, h * dh, (h + 1) * dh)
    qkv_r[me] = qkv[me]

    def send_qkv(peers):
        for peer in peers:
            go(ctx_copy(qkv.at[peer], qkv_r.at[me], qkv_ss.at[peer], qkv_rs.at[me], peer))

    pair_far = [lax.rem(pair + 2 * s, n) for s in range(1, n // 2)]
    down = lax.broadcasted_iota(jnp.int32, (block, block), 0)
    for j in range(n):
        entry = picked[0, j]
        kpos[j * block:(j + 1) * block] = down + jnp.where(entry >= 0, entry * block, FAR)
    own_proj.wait()

    def ctx_arrived(buf, ss, rs, peer):
        ctx_copy(buf.at[peer], buf.at[peer], ss.at[peer], rs.at[peer], peer).wait_recv()

    def dp_arrived(buf, ss, rs, peer):
        dp_copy(buf.at[peer], buf.at[peer], ss.at[peer], rs.at[peer], peer).wait_recv()

    for peer in dp_peers:
        dp_arrived(g_r, g_ss, g_rs, peer)

    def part(h):
        out = dot_nt(g_r[...].reshape(dn * block, dc), proj_r[h]).astype(bf16)
        agp_s[h] = out.reshape(dn, block, dh)
        for peer in dp_peers:
            go(dp_copy(agp_s.at[h, peer], agp_r.at[h, md], agp_ss.at[h, peer], agp_rs.at[h, md], peer))

    def finish(h):
        total = agp_s[h, md].astype(jnp.float32)
        for peer in dp_peers:
            dp_copy(agp_r.at[h, peer], agp_r.at[h, peer], agp_ss.at[h, peer], agp_rs.at[h, peer], peer).wait_recv()
            total = total + agp_r[h, peer].astype(jnp.float32)
        ag_s[h] = total.astype(bf16)
        if h is me:
            ag_r[me] = ag_s[me]
        else:
            go(ctx_copy(ag_s.at[h], ag_r.at[me], ag_ss.at[h], ag_rs.at[me], h))

    heads = [me, pair] + far + pair_far
    lag = 2
    for k, h in enumerate(heads):
        if k:
            ctx_arrived(proj_r, proj_ss, proj_rs, h)
        if 2 <= k < 2 + len(far):
            go(ctx_copy(proj_r.at[h], proj_r.at[h], fwd_ss.at[h], proj_rs.at[h], pair))
        part(h)
        if k == 1 + len(far):
            send_qkv(ctx_peers)
        if k >= lag:
            finish(heads[k - lag])
    for h in heads[-lag:]:
        finish(h)

    for peer in ctx_peers:
        ctx_arrived(qkv_r, qkv_ss, qkv_rs, peer)
    k_t[...] = transposed(qkv_r[:, 1].reshape(slots, dh))
    v_t[...] = transposed(qkv_r[:, 2].reshape(slots, dh))

    def send_pair(i, src, dst, ss, rs, own_sem):
        for half in range(2):
            peer = 2 * i + half

            @pl.when(peer != me)
            def _():
                ctx_copy(src.at[peer], dst.at[me], ss.at[peer], rs.at[me], peer).start()

            @pl.when(peer == me)
            def _():
                pltpu.make_async_copy(src.at[peer], dst.at[peer], own_sem).start()

    def forward(i, carry):
        q = qkv_r[pl.ds(2 * i, 2), 0].reshape(width, dh)
        k = qkv_r[:, 1].reshape(slots, dh)
        scores = dot_nt(k, q) * scale
        key_pos = kpos[...]
        key_pos = jnp.concatenate([key_pos, key_pos], axis=1)
        same = lax.broadcasted_iota(jnp.int32, (slots, width), 0) == (
            lax.broadcasted_iota(jnp.int32, (slots, width), 1) + i * width)
        lane = lax.broadcasted_iota(jnp.int32, (1, width), 1)
        first, second = picked[0, 2 * i], picked[0, 2 * i + 1]
        first = jnp.where(first >= 0, first * block, -FAR)
        second = jnp.where(second >= 0, (second - 1) * block, -FAR)
        query_pos = lane + jnp.where(lane < block, first, second)
        scores = jnp.where((key_pos <= query_pos) | same, scores, -1e30)
        e = jnp.exp(scores - jnp.max(scores, axis=0, keepdims=True))
        p = (e * (1.0 / jnp.sum(e, axis=0, keepdims=True))).astype(bf16)
        p_s[i] = p
        a_t = dot_nn(v_t[...], p)
        attn_t[i] = a_t.astype(bf16)
        attn_s[pl.ds(2 * i, 2)] = a_t.T.astype(bf16).reshape(2, block, dh)
        send_pair(i, attn_s, attn_r, attn_ss, attn_rs, loc.at[3])
        return carry

    lax.fori_loop(0, steps, forward, 0)

    for peer in ctx_peers:
        ctx_arrived(ag_r, ag_ss, ag_rs, peer)
    dk_acc[...] = jnp.zeros_like(dk_acc)
    dv_acc[...] = jnp.zeros_like(dv_acc)

    def backward(i, carry):
        q = qkv_r[pl.ds(2 * i, 2), 0].reshape(width, dh)
        v = qkv_r[:, 2].reshape(slots, dh)
        da = ag_r[pl.ds(2 * i, 2)].reshape(width, dh)
        delta = jnp.sum(da.astype(jnp.float32).T * attn_t[i].astype(jnp.float32), axis=0, keepdims=True)
        p = p_s[i]
        ds = (p.astype(jnp.float32) * (dot_nt(v, da) - delta)).astype(bf16)
        dq_t = dot_nn(k_t[...], ds) * scale
        dq_s[pl.ds(2 * i, 2)] = dq_t.T.astype(bf16).reshape(2, block, dh)
        send_pair(i, dq_s, dq_r, dq_ss, dq_rs, loc.at[4])
        dk_acc[...] += dot_nn(ds, q)
        dv_acc[...] += dot_nn(p, da)
        return carry

    early = steps // 2
    lax.fori_loop(0, early, backward, 0)
    for peer in ctx_peers:
        ctx_arrived(attn_r, attn_ss, attn_rs, peer)
    pltpu.make_async_copy(attn_s.at[me], attn_r.at[me], loc.at[3]).wait()
    twin = md + 1 - 2 * lax.rem(md, 2)
    dp_far = [lax.rem(md + 2 * s, dn) for s in range(1, dn // 2)]
    for peer in dp_far + [twin]:
        go(dp_copy(attn_r, attn_d.at[md], ad_ss.at[peer], ad_rs.at[md], peer))
    own_attn = pltpu.make_async_copy(attn_r, attn_d.at[md], loc.at[5])
    own_attn.start()
    lax.fori_loop(early, steps, backward, 0)

    dkv_s[:, 0] = (dk_acc[...] * scale).astype(bf16).reshape(n, block, dh)
    dkv_s[:, 1] = dv_acc[...].astype(bf16).reshape(n, block, dh)
    for peer in ctx_peers:
        go(ctx_copy(dkv_s.at[peer], dkv_r.at[me], dkv_ss.at[peer], dkv_rs.at[me], peer))
    dkv_r[me] = dkv_s[me]

    own_attn.wait()
    for peer in dp_far:
        dp_arrived(attn_d, ad_ss, ad_rs, peer)
        go(dp_copy(attn_d.at[peer], attn_d.at[peer], ad_fs.at[peer], ad_rs.at[peer], twin))
    for peer in [twin] + [lax.rem(twin + 2 * s, dn) for s in range(1, dn // 2)]:
        dp_arrived(attn_d, ad_ss, ad_rs, peer)

    def weight(h):
        heads = attn_d[:, h].reshape(dn * block, dh)
        return dot_nn(transposed(heads), g_r[...].reshape(dn * block, dc))

    side = lax.rem(me, 2)
    row = me // 2
    orders = [lax.rem(row + s, n // 2) for s in range(1, n // 2)] + [row]
    for a in orders:
        h = 2 * a + 1 - side
        w_s[h] = weight(h).astype(bf16)
        go(ctx_copy(w_s.at[h], w_y.at[a], w_ss.at[h], wy_rs.at[a], pair))

    def mix_step(j, carry):
        rows = jnp.concatenate(
            [attn_d[pl.ds(2 * j, 2), h].reshape(width, dh) for h in range(n)], axis=1)
        out = dot_nn(rows, proj_r[...].reshape(n * dh, dc))
        mix_s[pl.ds(2 * j, 2)] = out.astype(bf16).reshape(2, block, dc)
        return carry

    lax.fori_loop(0, dn // 2, mix_step, 0)
    for peer in dp_peers:
        go(dp_copy(mix_s.at[peer], mix_r.at[md], mix_ss.at[peer], mix_rs.at[md], peer))
    mix_r[md] = mix_s[md]

    for a in orders:
        h = 2 * a + side
        total = weight(h)
        ctx_copy(w_y.at[a], w_y.at[a], w_ss.at[h], wy_rs.at[a], pair).wait_recv()
        total = total + w_y[a].astype(jnp.float32)
        if a is row:
            w_out[...] = total
        else:
            w_s[h] = total.astype(bf16)
            go(ctx_copy(w_s.at[h], w_r.at[row], w_ss.at[h], w_rs.at[row], h))

    pltpu.make_async_copy(dq_s.at[me], dq_r.at[me], loc.at[4]).wait()
    for peer in ctx_peers:
        ctx_arrived(dq_r, dq_ss, dq_rs, peer)
    for peer in ctx_peers:
        ctx_arrived(dkv_r, dkv_ss, dkv_rs, peer)
    for a in orders[:-1]:
        ctx_copy(w_r.at[a], w_r.at[a], w_ss.at[a], w_rs.at[a], pair).wait_recv()
        w_out[...] += w_r[a].astype(jnp.float32)
    for peer in dp_peers:
        dp_arrived(mix_r, mix_ss, mix_rs, peer)

    for copy in sends:
        copy.wait_send()
    for peer in ctx_peers:
        ctx_copy(attn_s.at[peer], attn_r.at[me], attn_ss.at[peer], attn_rs.at[me], peer).wait_send()
        ctx_copy(dq_s.at[peer], dq_r.at[me], dq_ss.at[peer], dq_rs.at[me], peer).wait_send()


def shards(queries, keys, values, out_grad, chosen, proj):
    n = lax.axis_size("ctx")
    dn = lax.axis_size("dp")
    tokens = queries.shape[1]
    dh = queries.shape[2] // n
    dc = proj.shape[1]
    slots = n * BLOCK
    width = 2 * BLOCK
    steps = n // 2
    bf16, f32 = jnp.bfloat16, jnp.float32
    sem = pltpu.SemaphoreType.DMA
    vm = pltpu.VMEM
    blocks = (n, BLOCK, dh)
    scratch = [
        vm((n, 3, BLOCK, dh), bf16), vm((dn, BLOCK, dc), bf16), vm((slots, BLOCK), jnp.int32),
        vm((n, 3, BLOCK, dh), bf16), vm((dn, BLOCK, dc), bf16), vm((n, dh, dc), bf16),
        vm((n, dn, BLOCK, dh), bf16), vm((n, dn, BLOCK, dh), bf16), vm(blocks, bf16), vm(blocks, bf16),
        vm(blocks, bf16), vm(blocks, bf16), vm((dn,) + blocks, bf16), vm((steps, dh, width), bf16),
        vm((steps, slots, width), bf16), vm((dh, slots), bf16), vm((dh, slots), bf16),
        vm(blocks, bf16), vm((n, 2, BLOCK, dh), bf16), vm((slots, dh), f32), vm((slots, dh), f32),
        vm((n, dh, dc), bf16), vm((n // 2, dh, dc), bf16), vm((n // 2, dh, dc), bf16), vm((dn, BLOCK, dc), bf16),
    ]
    c, d = sem((n,)), sem((dn,))
    e = sem((n, dn))
    sems = [c, c, d, d, c, c, c, e, e, c, c, c, c, d, d, d, c, c, c, c, c, c, c, d, d, sem((6,))]
    vmem = pl.BlockSpec(memory_space=pltpu.VMEM)
    smem = pl.BlockSpec(memory_space=pltpu.SMEM)
    dq, dkv, weight_grad, mixed = pl.pallas_call(
        functools.partial(kernel, n, dn, 1.0 / math.sqrt(dh)),
        out_shape=(
            jax.ShapeDtypeStruct(blocks, bf16),
            jax.ShapeDtypeStruct((n, 2, BLOCK, dh), bf16),
            jax.ShapeDtypeStruct((dh, dc), f32),
            jax.ShapeDtypeStruct((dn, BLOCK, dc), bf16),
        ),
        in_specs=[smem] + [vmem] * 5,
        out_specs=[pl.BlockSpec(memory_space=pltpu.VMEM)] * 4,
        scratch_shapes=scratch + sems,
        compiler_params=pltpu.CompilerParams(
            collective_id=0, has_side_effects=True, vmem_limit_bytes=60 * 1024 * 1024),
    )(chosen, queries[0], keys[0], values[0], out_grad[0], proj)

    wide = jax.ShapeDtypeStruct((tokens, dn * dc), bf16)
    thin = jax.ShapeDtypeStruct((tokens, n * dh), bf16)
    out, q_grad, k_grad, v_grad, proj_grad = pl.pallas_call(
        functools.partial(place_kernel, n, dn, tokens // BLOCK),
        out_shape=(wide, thin, thin, thin, jax.ShapeDtypeStruct((dh, dc), f32)),
        in_specs=[smem] + [vmem] * 4,
        out_specs=[vmem] * 5,
    )(chosen, mixed, dq, dkv, weight_grad)
    return out[None], q_grad[None], k_grad[None], v_grad[None], proj_grad


def solution(mesh):
    rows = P("dp", "ctx", None)
    return jax.shard_map(
        shards,
        mesh=mesh,
        in_specs=(rows, rows, rows, rows, P("dp", None), P("ctx", "dp")),
        out_specs=(rows, rows, rows, rows, P("ctx", "dp")),
        check_vma=False,
    )
```
